32 devices in a mesh: box: 4 (over x, core), samp: 8 (over z, y).
Axes of the slice: x: 2, y: 2, z: 4, core: 2. Of those that a mesh axis runs over, the one named last changes fastest.
Arguments:
- child_out: float32 [1024, 2, 18432], P(('box', 'samp')), may hold values from -6 to 6
- child_octant: int32 [128, 8], P(('box', 'samp')), may hold values from 0 to 7, each once within a row
- theta_index: int32 [192, 4], replicated, may hold values from 0 to 95, as said below
- theta_weight: float32 [192, 4], replicated, may hold values from -0.2 to 0.6
- phi_index: int32 [384, 4], replicated, may hold values from 0 to 191, as said below
- phi_weight: float32 [384, 4], replicated, may hold values from -0.2 to 0.6
- shift_angle: float32 [8, 192, 384], replicated, may hold values from -3.140625 to 3.140625
- partner_src: int32 [128, 32], replicated, may hold values from 0 to 127
- partner_disp: int32 [128, 32], replicated, may hold values from 0 to 315
- translation: float32 [316, 2, 192, 384], P(None, None, 'samp'), may hold values from -0.75 to 0.75
Outputs:
- child_in: float32 [1024, 2, 18432], P(('box', 'samp'))
The draws below stay inside these ranges and needn't reach their ends.
Inputs may be any that keep to these rules, and one draw needn't show every extreme that they name: `theta_index`: four stencil indices for each fine theta sample, consecutive coarse samples near it, clipped to the ends so that they may repeat near the poles (repeated weights add). `phi_index`: four consecutive coarse phi samples near each fine phi sample, wrapping around in phi.
All inputs are finite; a program needn't handle non-finite values.
Results may differ from the reference program's by a relative error of at most 0.00007.
Values sent between devices are 32-bit elements; how exact they have to be, the bound alone decides.
A program may use at most 256 MiB of HBM per device.

```python
import jax
import jax.numpy as jnp
from jax import lax

NT1 = 96
NP1 = 192
NT2 = 192
NP2 = 384
NDISP = 316
NPART = 32
NB1 = 1024
NB2 = 128


def draw_theta_index(key, part):
    rows = jnp.arange(NT2, dtype=jnp.int32)
    offset = jax.random.randint(key, (NT2, 1), 0, 3, dtype=jnp.int32)
    start = (rows * NT1 // NT2)[:, None] - 2 + offset
    return jnp.clip(start + jnp.arange(4, dtype=jnp.int32)[None, :], 0, NT1 - 1).astype(jnp.int32)


def draw_phi_index(key, part):
    rows = jnp.arange(NP2, dtype=jnp.int32)
    offset = jax.random.randint(key, (NP2, 1), 0, 3, dtype=jnp.int32)
    start = (rows * NP1 // NP2)[:, None] - 2 + offset
    return jnp.mod(start + jnp.arange(4, dtype=jnp.int32)[None, :], NP1).astype(jnp.int32)


def place_ends(values, own_key, smallest, largest):
    dims = values.shape
    spot = [jax.random.randint(jax.random.fold_in(own_key, axis), (), 0, dims[axis]) for axis in range(len(dims))]
    values = values.at[tuple(spot)].set(smallest)
    longest = dims.index(max(dims))
    spot[longest] = (spot[longest] + 1) % dims[longest]
    return values.at[tuple(spot)].set(largest)


def level_of(key, dims, pieces, low, top_value):
    loudness = 1.0
    for dim, blocks in pieces:
        heights = jax.random.uniform(jax.random.fold_in(jax.random.fold_in(key, 6), dim), (blocks,), jnp.float32, low / len(pieces), top_value / len(pieces))
        loudness = loudness * jnp.repeat(jnp.exp(heights), dims[dim] // blocks).reshape((-1,) + (1,) * (len(dims) - 1 - dim))
    return loudness


def gaussian(key, extent, deviation, reach, pieces=(), kind=jnp.bfloat16):
    level = level_of(key, extent, pieces, -0.22, 0.18) if pieces else 1.0
    entries = jax.random.normal(key, extent, jnp.float32) * deviation * level
    return jnp.minimum(jnp.maximum(entries, -reach), reach).astype(kind)


def setup_inputs(seed: int = 0) -> dict:
    arg_keys = jax.random.split(jax.random.key(seed), 11)
    child_out = gaussian(arg_keys[0], (NB1, 2, NT1 * NP1), 1.0, 6.0, ((0, 32),), jnp.float32)
    child_octant = jax.vmap(lambda own: jax.random.permutation(own, 8))(jax.random.split(arg_keys[1], NB2)).reshape((NB2, 8)).astype(jnp.int32)
    theta_index = draw_theta_index(jax.random.fold_in(arg_keys[10], 71), 0)
    theta_weight = jnp.clip(jax.random.uniform(arg_keys[3], (NT2, 4), jnp.float32, -0.2, 0.6), -0.2, 0.6)
    phi_index = draw_phi_index(jax.random.fold_in(arg_keys[10], 71), 0)
    phi_weight = jnp.clip(jax.random.uniform(arg_keys[5], (NP2, 4), jnp.float32, -0.2, 0.6), -0.2, 0.6)
    shift_angle = jnp.clip(jax.random.uniform(arg_keys[6], (8, NT2, NP2), jnp.float32, -3.140625, 3.140625), -3.140625, 3.140625)
    partner_src = place_ends(jax.random.randint(arg_keys[7], (NB2, NPART), 0, NB2), jax.random.fold_in(arg_keys[7], 1), 0, NB2 - 1).astype(jnp.int32)
    partner_disp = place_ends(jax.random.randint(arg_keys[8], (NB2, NPART), 0, NDISP), jax.random.fold_in(arg_keys[8], 1), 0, NDISP - 1).astype(jnp.int32)
    translation = gaussian(arg_keys[9], (NDISP, 2, NT2, NP2), (1.0 / (2 * NPART) ** 0.5), 0.75, ((2, 8),), jnp.float32)
    return dict(child_out=child_out, child_octant=child_octant, theta_index=theta_index, theta_weight=theta_weight, phi_index=phi_index, phi_weight=phi_weight, shift_angle=shift_angle, partner_src=partner_src, partner_disp=partner_disp, translation=translation)


PRECISE = lax.Precision.HIGHEST


def stencil(index, weight, count):
    hits = (index[:, :, None] == jnp.arange(count, dtype=jnp.int32)[None, None, :]).astype(weight.dtype)
    return jnp.sum(weight[:, :, None] * hits, axis=1)


def spread(field, theta_mat, phi_mat):
    wider = jnp.einsum("czap,qp->czaq", field, phi_mat, precision=PRECISE)
    return jnp.einsum("ta,czaq->cztq", theta_mat, wider, precision=PRECISE)


def contract(field, theta_mat, phi_mat):
    narrow = jnp.einsum("ta,cztq->czaq", theta_mat, field, precision=PRECISE)
    return jnp.einsum("czaq,qp->czap", narrow, phi_mat, precision=PRECISE)


def rotate(field, cosine, sine_part):
    real_part = field[:, 0]
    imag_part = field[:, 1]
    return jnp.stack([real_part * cosine - imag_part * sine_part, real_part * sine_part + imag_part * cosine], axis=1)


def rotate_back(field, cosine, sine_part):
    real_part = field[:, 0]
    imag_part = field[:, 1]
    return jnp.stack([real_part * cosine + imag_part * sine_part, imag_part * cosine - real_part * sine_part], axis=1)


def reference(child_out, child_octant, theta_index, theta_weight, phi_index, phi_weight, shift_angle, partner_src, partner_disp, translation):
    theta_mat = stencil(theta_index, theta_weight, NT1)
    phi_mat = stencil(phi_index, phi_weight, NP1)
    cos_table = jnp.cos(shift_angle)
    sin_table = jnp.sin(shift_angle)
    children = child_out.reshape(NB2, 8, 2, NT1, NP1)

    def aggregate(items):
        kids, octants = items
        cos_sel = jnp.take(cos_table, octants, axis=0)
        sin_sel = jnp.take(sin_table, octants, axis=0)
        fine_child = rotate(spread(kids, theta_mat, phi_mat), cos_sel, sin_sel)
        return jnp.sum(fine_child, axis=0)

    parent_out = lax.map(aggregate, (children, child_octant))

    def translate_one(items):
        sources, displacements = items
        picked = jnp.take(parent_out, sources, axis=0)
        operators = jnp.take(translation, displacements, axis=0)
        real_sum = jnp.sum(operators[:, 0] * picked[:, 0] - operators[:, 1] * picked[:, 1], axis=0)
        imag_sum = jnp.sum(operators[:, 0] * picked[:, 1] + operators[:, 1] * picked[:, 0], axis=0)
        return jnp.stack([real_sum, imag_sum], axis=0)

    parent_in = lax.map(translate_one, (partner_src, partner_disp))

    def disaggregate(items):
        parent, octants = items
        cos_sel = jnp.take(cos_table, octants, axis=0)
        sin_sel = jnp.take(sin_table, octants, axis=0)
        repeated = jnp.broadcast_to(parent[None], (8,) + parent.shape)
        return contract(rotate_back(repeated, cos_sel, sin_sel), theta_mat, phi_mat)

    child_in = lax.map(disaggregate, (parent_in, child_octant))
    return child_in.reshape(NB1, 2, NT1 * NP1)
```

```python
import functools

import jax
import jax.numpy as jnp
from jax import lax
from jax.experimental import pallas as pl
from jax.experimental.pallas import tpu as pltpu
from jax.sharding import PartitionSpec as P

NT1 = 96
NP1 = 192
LANES = 128
MESH = pl.DeviceIdType.MESH
VMEM_LIMIT = 62 * 1024 * 1024


def stencil(index, weight, count):
    hits = (index[:, :, None] == jnp.arange(count, dtype=jnp.int32)[None, None, :]).astype(
        weight.dtype
    )
    return jnp.sum(weight[:, :, None] * hits, axis=1)


def split(values):
    high = values.astype(jnp.bfloat16)
    low = (values - high.astype(jnp.float32)).astype(jnp.bfloat16)
    return high, low


def dot(left, right):
    return jnp.dot(left, right, preferred_element_type=jnp.float32)


def dot3(left, right):
    return dot(left[0], right[0]) + dot(left[1], right[0]) + dot(left[0], right[1])


def aggregate_kernel(
    octant, child, cosine, sine, top_hi, top_lo, low_hi, low_lo, theta, out, wide
):
    parent = pl.program_id(0)
    kids, parts, half, width = child.shape
    field = child[...].reshape(kids * parts * half, width)
    edge = top_hi.shape[0]
    even = split(dot3(split(field[:, :edge]), (top_hi[...], top_lo[...])))
    odd = split(dot3(split(field[:, width - edge :]), (low_hi[...], low_lo[...])))
    for slot, piece in enumerate((even[0], odd[0], even[1], odd[1], even[0], odd[0])):
        wide[:, slot * half : (slot + 1) * half, :] = piece.reshape(kids * parts, half, piece.shape[1])
    out[...] = jnp.zeros_like(out)

    def one_child(kid, carry):
        spot = octant[parent * kids + kid]
        for chunk in range(out.shape[0]):
            lanes = slice(chunk * LANES, (chunk + 1) * LANES)
            real = dot(theta[...], wide[kid * 2, :, lanes])
            imag = dot(theta[...], wide[kid * 2 + 1, :, lanes])
            cos_part = cosine[spot, :, lanes]
            sin_part = sine[spot, :, lanes]
            out[chunk, 0, 0] += real * cos_part - imag * sin_part
            out[chunk, 0, 1] += real * sin_part + imag * cos_part
        return carry

    lax.fori_loop(0, kids, one_child, 0)


def disaggregate_kernel(
    octant, field, cosine, sine, theta_hi, theta_lo, left_hi, left_lo, right_hi, right_lo, out, even_hi, even_lo, odd_hi, odd_lo
):
    parent = pl.program_id(0)
    kids, parts, half, width = out.shape

    def one_child(kid, carry):
        spot = octant[parent * kids + kid]
        for chunk in range(field.shape[0]):
            lanes = slice(chunk * LANES, (chunk + 1) * LANES)
            real = field[chunk, 0, 0]
            imag = field[chunk, 0, 1]
            cos_part = cosine[spot, :, lanes]
            sin_part = sine[spot, :, lanes]
            turned = jnp.concatenate(
                [real * cos_part + imag * sin_part, imag * cos_part - real * sin_part], axis=1
            )
            narrow = split(dot3((theta_hi[...], theta_lo[...]), split(turned)))
            for part in range(parts):
                piece = slice(part * LANES, (part + 1) * LANES)
                even_hi[kid * 2 + part, :, lanes] = narrow[0][:half, piece]
                odd_hi[kid * 2 + part, :, lanes] = narrow[0][half:, piece]
                even_lo[kid * 2 + part, :, lanes] = narrow[1][:half, piece]
                odd_lo[kid * 2 + part, :, lanes] = narrow[1][half:, piece]
        return carry

    lax.fori_loop(0, kids, one_child, 0)

    def flat(ref):
        return ref[...].reshape(kids * parts * half, ref.shape[2])

    left = dot3((flat(even_hi), flat(even_lo)), (left_hi[...], left_lo[...]))
    right = dot3((flat(odd_hi), flat(odd_lo)), (right_hi[...], right_lo[...]))
    edge = left.shape[1]
    shared = 2 * edge - width
    joined = jnp.concatenate(
        [left[:, : edge - shared], left[:, edge - shared :] + right[:, :shared], right[:, shared:]], axis=1
    )
    out[...] = joined.reshape(out.shape)


def exchange_kernel(
    boxes, samps, partners, src_rows, disp_rows, outgoing, table, incoming, *scratch
):
    chunks = outgoing.shape[0]
    sources = scratch[:chunks]
    operators = scratch[chunks : 2 * chunks]
    results = scratch[2 * chunks : 3 * chunks]
    load_sem, own_sem, out_send, out_recv, box_send, box_recv, back_own, back_send, back_recv = scratch[3 * chunks :]
    group = lax.axis_index("box")
    me = lax.axis_index("samp")
    per_device = outgoing.shape[1]
    bits = [1 << i for i in range(boxes.bit_length() - 1)][::-1]

    def mate(bit):
        return group + bit - 2 * bit * lax.rem(lax.div(group, bit), 2)

    barrier = pltpu.get_barrier_semaphore()
    for step in range(1, samps):
        pl.semaphore_signal(barrier, inc=1, device_id=(group, lax.rem(me + step, samps)), device_id_type=MESH)
    for bit in bits:
        pl.semaphore_signal(barrier, inc=1, device_id=(mate(bit), me), device_id_type=MESH)

    def load(chunk):
        return pltpu.make_async_copy(
            table.at[:, :, :, pl.ds(chunk * LANES, LANES)], operators[chunk], load_sem.at[chunk]
        )

    def keep(chunk):
        return pltpu.make_async_copy(
            outgoing.at[chunk, :, :, me], sources[chunk].at[group, me], own_sem.at[chunk]
        )

    def out_copy(chunk, peer, owner):
        return pltpu.make_async_remote_copy(
            src_ref=outgoing.at[chunk, :, :, peer],
            dst_ref=sources[chunk].at[group, owner],
            send_sem=out_send.at[chunk, peer],
            recv_sem=out_recv.at[chunk, owner],
            device_id=(group, peer),
            device_id_type=MESH,
        )

    def back_copy(chunk, peer, owner):
        return pltpu.make_async_remote_copy(
            src_ref=results[chunk].at[peer],
            dst_ref=incoming.at[chunk, :, :, owner],
            send_sem=back_send.at[chunk, peer],
            recv_sem=back_recv.at[chunk, owner],
            device_id=(group, peer),
            device_id_type=MESH,
        )

    def back_keep(chunk):
        return pltpu.make_async_copy(
            results[chunk].at[me], incoming.at[chunk, :, :, me], back_own.at[chunk]
        )

    def box_plan():
        plan = []
        held = [0]
        for bit in bits:
            plan.append((bit, list(held)))
            held = held + [h + bit for h in held]
        return plan

    plan = box_plan()

    def owner_of(mask):
        spot = group
        for bit in bits:
            if mask & bit:
                spot = spot + bit - 2 * bit * lax.rem(lax.div(group, bit), 2)
        return spot

    def hop(chunk, bit, mask):
        return pltpu.make_async_remote_copy(
            src_ref=sources[chunk].at[owner_of(mask)],
            dst_ref=sources[chunk].at[owner_of(mask)],
            send_sem=box_send.at[chunk, mask + bit],
            recv_sem=box_recv.at[chunk, mask + bit],
            device_id=(mate(bit), me),
            device_id_type=MESH,
        )

    def hop_arrival(chunk, mask):
        spot = owner_of(mask)
        return pltpu.make_async_remote_copy(
            src_ref=sources[chunk].at[spot],
            dst_ref=sources[chunk].at[spot],
            send_sem=box_send.at[chunk, mask],
            recv_sem=box_recv.at[chunk, mask],
            device_id=(mate(bits[0]), me),
            device_id_type=MESH,
        )

    for chunk in range(chunks):
        keep(chunk).start()
    for chunk in range(chunks):
        load(chunk).start()
    pl.semaphore_wait(barrier, samps - 1 + len(bits))

    for chunk in range(chunks):

        def send_out(step, carry, chunk=chunk):
            out_copy(chunk, lax.rem(me + step, samps), me).start()
            return carry

        lax.fori_loop(1, samps, send_out, 0)

    def arrive_and_share(chunk):
        def arrived(step, carry):
            peer = lax.rem(me + samps - step, samps)
            out_copy(chunk, peer, peer).wait_recv()
            return carry

        keep(chunk).wait()
        lax.fori_loop(1, samps, arrived, 0)
        for bit, held in plan:
            hop(chunk, bit, 0).start()

    def pass_on(chunk):
        for position, (bit, held) in enumerate(plan):
            for mask in held:
                if mask == 0:
                    continue
                hop(chunk, bit, mask).start()
            if position + 1 < len(plan):
                for mask in [h + bit for h in held]:
                    hop_arrival(chunk, mask).wait_recv()

    def translate(chunk):
        last_bit, last_held = plan[-1]
        for mask in [h + last_bit for h in last_held]:
            hop_arrival(chunk, mask).wait_recv()
        load(chunk).wait()

        def receivers(step, carry):
            peer = lax.rem(me + 1 + step, samps)

            def one(slot, inner):
                row = (peer * per_device + slot) * partners
                real = jnp.zeros(results[chunk].shape[3:], jnp.float32)
                imag = jnp.zeros(results[chunk].shape[3:], jnp.float32)
                for q in range(partners):
                    source = src_rows[row + q]
                    which = disp_rows[row + q]
                    here = lax.div(source, samps * per_device)
                    rest = lax.rem(source, samps * per_device)
                    from_samp = lax.div(rest, per_device)
                    from_slot = lax.rem(rest, per_device)
                    a = sources[chunk][here, from_samp, from_slot, 0]
                    b = sources[chunk][here, from_samp, from_slot, 1]
                    c = operators[chunk][which, 0]
                    d = operators[chunk][which, 1]
                    real = real + (c * a - d * b)
                    imag = imag + (c * b + d * a)
                results[chunk][peer, slot, 0] = real
                results[chunk][peer, slot, 1] = imag
                return inner

            lax.fori_loop(0, per_device, one, 0)

            @pl.when(step > 0)
            def _():
                peer_before = lax.rem(me + step, samps)
                back_copy(chunk, peer_before, me).start()

            return carry

        lax.fori_loop(0, samps, receivers, 0)
        back_keep(chunk).start()

    arrive_and_share(0)
    for chunk in range(chunks):
        if chunk + 1 < chunks:
            arrive_and_share(chunk + 1)
        pass_on(chunk)
        translate(chunk)

    for chunk in range(chunks):

        def finish(step, carry, chunk=chunk):
            there = lax.rem(me + step, samps)
            out_copy(chunk, there, there).wait_send()
            back_copy(chunk, there, there).wait_send()
            back_copy(chunk, there, there).wait_recv()
            return carry

        lax.fori_loop(1, samps, finish, 0)
        for bit, held in plan:
            for mask in held:
                hop(chunk, bit, mask).wait_send()
        back_keep(chunk).wait()


def local(
    boxes,
    samps,
    child_out,
    child_octant,
    theta_index,
    theta_weight,
    phi_index,
    phi_weight,
    shift_angle,
    partner_src,
    partner_disp,
    translation,
):
    child_count, parts, samples = child_out.shape
    parents, kids = child_octant.shape
    rows2, cols2 = shift_angle.shape[1:]
    partners = partner_src.shape[1]
    theta_rows = rows2 // samps
    chunks = cols2 // LANES
    half = NT1 // 2
    width = 2 * NP1
    edge = -(-NP1 // LANES) * LANES
    gap = edge - NP1

    theta_mat = stencil(theta_index, theta_weight, NT1)
    phi_mat = stencil(phi_index, phi_weight, NP1)
    theta_mat = jnp.concatenate([theta_mat[:, 0::2], theta_mat[:, 1::2]], axis=1)

    def parts_of(matrix):
        high = lax.reduce_precision(matrix, 8, 7)
        low = lax.reduce_precision(matrix - high, 8, 7)
        return high.astype(jnp.bfloat16), low.astype(jnp.bfloat16)

    theta_hi, theta_lo = parts_of(theta_mat)
    phi_hi, phi_lo = parts_of(phi_mat)
    theta_all = jnp.concatenate([theta_hi, theta_hi, theta_lo], axis=1)
    before = ((0, 0), (gap, 0))
    after = ((0, 0), (0, gap))
    left = [jnp.pad(m, after) for m in (phi_hi, phi_lo)]
    right = [jnp.pad(m, before) for m in (phi_hi, phi_lo)]
    cosine = jnp.cos(shift_angle)
    sine = jnp.sin(shift_angle)
    octants = child_octant.reshape(-1)
    child = child_out.reshape(child_count, parts, half, width)

    def whole(array):
        return pl.BlockSpec(array.shape, lambda *_: (0,) * array.ndim)

    child_spec = pl.BlockSpec((kids, parts, half, width), lambda i, _: (i, 0, 0, 0))
    parent_spec = pl.BlockSpec((chunks, 1, parts, rows2, LANES), lambda i, _: (0, i, 0, 0, 0))

    extra = [left[0].T, left[1].T, right[0].T, right[1].T, theta_all]
    parent_out = pl.pallas_call(
        aggregate_kernel,
        out_shape=jax.ShapeDtypeStruct((chunks, parents, parts, rows2, LANES), jnp.float32),
        grid_spec=pltpu.PrefetchScalarGridSpec(
            num_scalar_prefetch=1,
            grid=(parents,),
            in_specs=[child_spec, whole(cosine), whole(sine)] + [whole(m) for m in extra],
            out_specs=parent_spec,
            scratch_shapes=[pltpu.VMEM((kids * parts, 3 * NT1, cols2), jnp.bfloat16)],
        ),
        compiler_params=pltpu.CompilerParams(vmem_limit_bytes=VMEM_LIMIT),
    )(octants, child, cosine, sine, *extra)

    group_rows = parents * samps
    start = lax.axis_index("box") * group_rows
    src_rows = lax.dynamic_slice_in_dim(partner_src, start, group_rows, 0).reshape(-1)
    disp_rows = lax.dynamic_slice_in_dim(partner_disp, start, group_rows, 0).reshape(-1)
    block = (parents, parts, theta_rows, LANES)
    anywhere = pl.BlockSpec(memory_space=pl.ANY)
    table = pl.BlockSpec(memory_space=pltpu.SMEM)
    outgoing = parent_out.reshape(chunks, parents, parts, samps, theta_rows, LANES)
    incoming = pl.pallas_call(
        functools.partial(exchange_kernel, boxes, samps, partners),
        out_shape=jax.ShapeDtypeStruct(outgoing.shape, jnp.float32),
        in_specs=[table, table, anywhere, anywhere],
        out_specs=anywhere,
        scratch_shapes=[pltpu.VMEM((boxes, samps) + block, jnp.float32)] * chunks
        + [pltpu.VMEM(translation.shape[:3] + (LANES,), jnp.float32)] * chunks
        + [pltpu.VMEM((samps,) + block, jnp.float32)] * chunks
        + [
            pltpu.SemaphoreType.DMA((chunks,)),
            pltpu.SemaphoreType.DMA((chunks,)),
            pltpu.SemaphoreType.DMA((chunks, samps)),
            pltpu.SemaphoreType.DMA((chunks, samps)),
            pltpu.SemaphoreType.DMA((chunks, boxes)),
            pltpu.SemaphoreType.DMA((chunks, boxes)),
            pltpu.SemaphoreType.DMA((chunks,)),
            pltpu.SemaphoreType.DMA((chunks, samps)),
            pltpu.SemaphoreType.DMA((chunks, samps)),
        ],
        compiler_params=pltpu.CompilerParams(
            collective_id=0, has_side_effects=True, vmem_limit_bytes=VMEM_LIMIT
        ),
    )(src_rows, disp_rows, outgoing, translation)
    parent_in = incoming.reshape(chunks, parents, parts, rows2, LANES)

    extra = [theta_hi.T, theta_lo.T, left[0], left[1], right[0], right[1]]
    child_in = pl.pallas_call(
        disaggregate_kernel,
        out_shape=jax.ShapeDtypeStruct((child_count, parts, half, width), jnp.float32),
        grid_spec=pltpu.PrefetchScalarGridSpec(
            num_scalar_prefetch=1,
            grid=(parents,),
            in_specs=[parent_spec, whole(cosine), whole(sine)] + [whole(m) for m in extra],
            out_specs=child_spec,
            scratch_shapes=[pltpu.VMEM((kids * parts, half, cols2), jnp.bfloat16)] * 4,
        ),
        compiler_params=pltpu.CompilerParams(vmem_limit_bytes=VMEM_LIMIT),
    )(octants, parent_in, cosine, sine, *extra)
    return child_in.reshape(child_count, parts, samples)


def solution(mesh):
    in_specs = (
        P(("box", "samp"), None, None),
        P(("box", "samp"), None),
        P(),
        P(),
        P(),
        P(),
        P(),
        P(),
        P(),
        P(None, None, "samp", None),
    )
    out_specs = P(("box", "samp"), None, None)
    body = functools.partial(local, mesh.shape["box"], mesh.shape["samp"])
    return jax.shard_map(body, mesh=mesh, in_specs=in_specs, out_specs=out_specs, check_vma=False)
```

```python
import functools

import jax
import jax.numpy as jnp
from jax import lax
from jax.experimental import pallas as pl
from jax.experimental.pallas import tpu as pltpu
from jax.sharding import PartitionSpec as P

NT1 = 96
NP1 = 192
LANES = 128
MESH = pl.DeviceIdType.MESH
VMEM_LIMIT = 62 * 1024 * 1024


def split(values):
    high = values.astype(jnp.bfloat16)
    low = (values - high.astype(jnp.float32)).astype(jnp.bfloat16)
    return high, low


def dot(left, right):
    return jnp.dot(left, right, preferred_element_type=jnp.float32)


def stencil(wanted, index, weight, axis):
    total = jnp.zeros(wanted.shape, jnp.float32)
    for j in range(index.shape[axis]):
        one = slice(j, j + 1)
        spot = (slice(None), one) if axis == 1 else (one, slice(None))
        total = total + jnp.where(wanted == index[spot], weight[spot], 0.0)
    return total


def iota(shape, axis):
    return lax.broadcasted_iota(jnp.int32, shape, axis)


HALF_PI = (1.5703125, 4.837512969970703e-4, 7.54978995489188e-8)


def cos_sin(angle):
    turns = jnp.floor(angle * 0.6366197723675814 + 0.5)
    rest = ((angle - turns * HALF_PI[0]) - turns * HALF_PI[1]) - turns * HALF_PI[2]
    square = rest * rest
    sine = -1.9515295891e-4 * square + 8.3321608736e-3
    sine = (sine * square - 1.6666654611e-1) * square * rest + rest
    cosine = 2.443315711809948e-5 * square - 1.388731625493765e-3
    cosine = (cosine * square + 4.166664568298827e-2) * square * square - 0.5 * square + 1.0
    half = jnp.floor(turns * 0.5)
    odd = turns - 2.0 * half > 0.5
    flip = half - 2.0 * jnp.floor(half * 0.5) > 0.5
    sin_part = jnp.where(odd, cosine, sine)
    cos_part = jnp.where(odd, -sine, cosine)
    return jnp.where(flip, -cos_part, cos_part), jnp.where(flip, -sin_part, sin_part)


def step_kernel(
    boxes,
    samps,
    partners,
    src_rows,
    disp_rows,
    octant,
    theta_index,
    theta_weight,
    theta_index_t,
    theta_weight_t,
    phi_index,
    phi_weight,
    phi_index_t,
    phi_weight_t,
    child,
    angle,
    table,
    result,
    field,
    wide,
    wide_out,
    grid_sum,
    theta_up,
    theta_down,
    *scratch,
):
    count, parts, half, width = child.shape
    chunks = angle.shape[2] // LANES
    rows2 = angle.shape[1]
    sources = scratch[:chunks]
    operators = scratch[chunks : 2 * chunks]
    results = scratch[2 * chunks : 3 * chunks]
    outgoing = scratch[3 * chunks : 4 * chunks]
    incoming = scratch[4 * chunks : 5 * chunks]
    cosines = scratch[5 * chunks : 6 * chunks]
    sines = scratch[6 * chunks : 7 * chunks]
    (
        child_sem,
        angle_sem,
        result_sem,
        load_sem,
        own_sem,
        out_send,
        out_recv,
        box_send,
        box_recv,
        back_own,
        back_send,
        back_recv,
    ) = scratch[7 * chunks :]
    per_device = outgoing[0].shape[0]
    kids = count // per_device
    theta_rows = rows2 // samps
    edge = -(-(width // 2) // LANES) * LANES
    gap = edge - width // 2
    group = lax.axis_index("box")
    me = lax.axis_index("samp")
    bits = [1 << i for i in range(boxes.bit_length() - 1)][::-1]

    def mate(bit):
        return group + bit - 2 * bit * lax.rem(lax.div(group, bit), 2)

    barrier = pltpu.get_barrier_semaphore()
    for step in range(1, samps):
        pl.semaphore_signal(barrier, inc=1, device_id=(group, lax.rem(me + step, samps)), device_id_type=MESH)
    for bit in bits:
        pl.semaphore_signal(barrier, inc=1, device_id=(mate(bit), me), device_id_type=MESH)

    def load(chunk):
        return pltpu.make_async_copy(
            table.at[:, :, :, pl.ds(chunk * LANES, LANES)], operators[chunk], load_sem.at[chunk]
        )

    def keep(chunk):
        return pltpu.make_async_copy(
            outgoing[chunk].at[:, :, me], sources[chunk].at[group, me], own_sem.at[chunk]
        )

    def out_copy(chunk, peer, owner):
        return pltpu.make_async_remote_copy(
            src_ref=outgoing[chunk].at[:, :, peer],
            dst_ref=sources[chunk].at[group, owner],
            send_sem=out_send.at[chunk, peer],
            recv_sem=out_recv.at[chunk, owner],
            device_id=(group, peer),
            device_id_type=MESH,
        )

    def back_copy(chunk, peer, owner):
        return pltpu.make_async_remote_copy(
            src_ref=results[chunk].at[peer],
            dst_ref=incoming[chunk].at[:, :, owner],
            send_sem=back_send.at[chunk, peer],
            recv_sem=back_recv.at[chunk, owner],
            device_id=(group, peer),
            device_id_type=MESH,
        )

    def back_keep(chunk):
        return pltpu.make_async_copy(
            results[chunk].at[me], incoming[chunk].at[:, :, me], back_own.at[chunk]
        )

    def box_plan():
        plan = []
        held = [0]
        for bit in bits:
            plan.append((bit, list(held)))
            held = held + [h + bit for h in held]
        return plan

    plan = box_plan()

    def owner_of(mask):
        spot = group
        for bit in bits:
            if mask & bit:
                spot = spot + bit - 2 * bit * lax.rem(lax.div(group, bit), 2)
        return spot

    def hop(chunk, bit, mask):
        return pltpu.make_async_remote_copy(
            src_ref=sources[chunk].at[owner_of(mask)],
            dst_ref=sources[chunk].at[owner_of(mask)],
            send_sem=box_send.at[chunk, mask + bit],
            recv_sem=box_recv.at[chunk, mask + bit],
            device_id=(mate(bit), me),
            device_id_type=MESH,
        )

    def hop_arrival(chunk, mask):
        spot = owner_of(mask)
        return pltpu.make_async_remote_copy(
            src_ref=sources[chunk].at[spot],
            dst_ref=sources[chunk].at[spot],
            send_sem=box_send.at[chunk, mask],
            recv_sem=box_recv.at[chunk, mask],
            device_id=(mate(bits[0]), me),
            device_id_type=MESH,
        )

    def load_angle(chunk):
        return pltpu.make_async_copy(
            angle.at[:, :, pl.ds(chunk * LANES, LANES)], cosines[chunk], angle_sem.at[chunk]
        )

    load_child = pltpu.make_async_copy(child, field, child_sem)

    def give(parent):
        rows = pl.ds(parent * kids, kids)
        return pltpu.make_async_copy(field.at[rows], result.at[rows], result_sem.at[parent])

    def build_theta():
        column = iota(theta_up.shape, 1)
        spot = lax.rem(column, 2 * half)
        sample = jnp.where(spot < half, 2 * spot, 2 * (spot - half) + 1)
        high, low = split(stencil(sample, theta_index, theta_weight, 1))
        theta_up[...] = jnp.where(column < 4 * half, high.astype(jnp.float32), low.astype(jnp.float32)).astype(
            jnp.bfloat16
        )
        spot = iota((2 * half, rows2), 0)
        sample = jnp.where(spot < half, 2 * spot, 2 * (spot - half) + 1)
        high, low = split(stencil(sample, theta_index_t, theta_weight_t, 0))
        theta_down[: 2 * half] = high
        theta_down[2 * half :] = low

    def turn(chunk):
        def one(spot, carry):
            cos_part, sin_part = cos_sin(cosines[chunk][spot])
            cosines[chunk][spot] = cos_part
            sines[chunk][spot] = sin_part
            return carry

        lax.fori_loop(0, cosines[chunk].shape[0], one, 0)

    def aggregate(chunk):
        lanes = slice(chunk * LANES, (chunk + 1) * LANES)
        sample = iota((edge, LANES), 0)
        mats = []
        for shift in (0, gap):
            high, low = split(stencil(sample - shift, phi_index_t[:, lanes], phi_weight_t[:, lanes], 0))
            mats.append(jnp.concatenate([high, low], axis=1))

        def one_parent(parent, carry):
            block = field[pl.ds(parent * kids, kids)].reshape(kids * parts * half, width)
            pieces = []
            for mat, start in zip(mats, (0, width - edge)):
                high, low = split(block[:, start : start + edge])
                both = dot(high, mat)
                pieces.append(split(both[:, :LANES] + (both[:, LANES:] + dot(low, mat[:, :LANES]))))
            even, odd = pieces
            for slot, piece in enumerate((even[0], odd[0], even[1], odd[1], even[0], odd[0])):
                piece = piece.reshape(kids, parts, half, LANES)
                for part in range(parts):
                    wide[:, slot * half : (slot + 1) * half, part * LANES : (part + 1) * LANES] = piece[:, part]
            grid_sum[...] = jnp.zeros_like(grid_sum)

            def one_child(kid, inner):
                spot = octant[parent * kids + kid]
                fine = dot(theta_up[...], wide[kid])
                real, imag = fine[:, :LANES], fine[:, LANES:]
                cos_part = cosines[chunk][spot]
                sin_part = sines[chunk][spot]
                grid_sum[0] += real * cos_part - imag * sin_part
                grid_sum[1] += real * sin_part + imag * cos_part
                return inner

            lax.fori_loop(0, kids, one_child, 0)
            for part in range(parts):
                for owner in range(samps):
                    outgoing[chunk][parent, part, owner] = grid_sum[
                        part, owner * theta_rows : (owner + 1) * theta_rows
                    ]
            return carry

        lax.fori_loop(0, per_device, one_parent, 0)

    def disaggregate(chunk, first, last):
        rows = slice(chunk * LANES, (chunk + 1) * LANES)
        sample = iota((LANES, edge), 1)
        mats = []
        for shift in (0, gap):
            high, low = split(stencil(sample - shift, phi_index[rows], phi_weight[rows], 1))
            mats.append((jnp.concatenate([high, high], axis=0), low))

        def one_parent(parent, carry):
            for part in range(parts):
                for owner in range(samps):
                    grid_sum[part, owner * theta_rows : (owner + 1) * theta_rows] = incoming[chunk][
                        parent, part, owner
                    ]

            def one_child(kid, inner):
                spot = octant[parent * kids + kid]
                real, imag = grid_sum[0], grid_sum[1]
                cos_part = cosines[chunk][spot]
                sin_part = sines[chunk][spot]
                turned = jnp.concatenate(
                    [real * cos_part + imag * sin_part, imag * cos_part - real * sin_part], axis=1
                )
                high, low = split(turned)
                both = dot(theta_down[...], high)
                narrow = both[: 2 * half] + (both[2 * half :] + dot(theta_down[: 2 * half], low))
                for place, piece in enumerate(split(narrow)):
                    for parity in range(2):
                        for part in range(parts):
                            wide_out[
                                parity, kid * parts + part, :, place * LANES : (place + 1) * LANES
                            ] = piece[parity * half : (parity + 1) * half, part * LANES : (part + 1) * LANES]
                return inner

            lax.fori_loop(0, kids, one_child, 0)
            ends = []
            for parity in range(2):
                flat = wide_out[parity].reshape(kids * parts * half, 2 * LANES)
                ends.append(dot(flat, mats[parity][0]) + dot(flat[:, :LANES], mats[parity][1]))
            left, right = ends
            shared = 2 * edge - width
            joined = jnp.concatenate(
                [left[:, : edge - shared], left[:, edge - shared :] + right[:, :shared], right[:, shared:]],
                axis=1,
            ).reshape(kids, parts, half, width)
            spot = pl.ds(parent * kids, kids)
            if first:
                field[spot] = joined
            else:
                field[spot] += joined
            if last:

                @pl.when(parent > 0)
                def _():
                    give(parent - 1).start()

            return carry

        lax.fori_loop(0, per_device, one_parent, 0)

    def send_out(chunk):
        def one(step, carry):
            out_copy(chunk, lax.rem(me + step, samps), me).start()
            return carry

        lax.fori_loop(1, samps, one, 0)
        keep(chunk).start()

    load_child.start()
    for chunk in range(chunks):
        load_angle(chunk).start()
    for chunk in range(chunks):
        load(chunk).start()
    build_theta()
    load_angle(0).wait()
    turn(0)
    load_child.wait()
    aggregate(0)
    for chunk in range(1, chunks):
        load_angle(chunk).wait()
        turn(chunk)
        if chunk == 1:
            pl.semaphore_wait(barrier, samps - 1 + len(bits))
        send_out(chunk - 1)
        aggregate(chunk)

    def arrive_and_share(chunk):
        def arrived(step, carry):
            peer = lax.rem(me + samps - step, samps)
            out_copy(chunk, peer, peer).wait_recv()
            return carry

        keep(chunk).wait()
        lax.fori_loop(1, samps, arrived, 0)
        for bit, held in plan:
            hop(chunk, bit, 0).start()

    def pass_on(chunk):
        for position, (bit, held) in enumerate(plan):
            for mask in held:
                if mask == 0:
                    continue
                hop(chunk, bit, mask).start()
            if position + 1 < len(plan):
                for mask in [h + bit for h in held]:
                    hop_arrival(chunk, mask).wait_recv()

    def translate(chunk):
        last_bit, last_held = plan[-1]
        for mask in [h + last_bit for h in last_held]:
            hop_arrival(chunk, mask).wait_recv()
        load(chunk).wait()

        def receivers(step, carry):
            peer = lax.rem(me + 1 + step, samps)

            def one(slot, inner):
                row = (peer * per_device + slot) * partners
                real = jnp.zeros(results[chunk].shape[3:], jnp.float32)
                imag = jnp.zeros(results[chunk].shape[3:], jnp.float32)
                for q in range(partners):
                    source = src_rows[row + q]
                    which = disp_rows[row + q]
                    here = lax.div(source, samps * per_device)
                    rest = lax.rem(source, samps * per_device)
                    from_samp = lax.div(rest, per_device)
                    from_slot = lax.rem(rest, per_device)
                    a = sources[chunk][here, from_samp, from_slot, 0]
                    b = sources[chunk][here, from_samp, from_slot, 1]
                    c = operators[chunk][which, 0]
                    d = operators[chunk][which, 1]
                    real = real + (c * a - d * b)
                    imag = imag + (c * b + d * a)
                results[chunk][peer, slot, 0] = real
                results[chunk][peer, slot, 1] = imag
                return inner

            lax.fori_loop(0, per_device, one, 0)

            @pl.when(step > 0)
            def _():
                peer_before = lax.rem(me + step, samps)
                back_copy(chunk, peer_before, me).start()

            return carry

        lax.fori_loop(0, samps, receivers, 0)

    def returned(chunk):
        def one(step, carry):
            there = lax.rem(me + samps - step, samps)
            back_copy(chunk, there, there).wait_recv()
            return carry

        lax.fori_loop(1, samps, one, 0)
        back_keep(chunk).wait()

    arrive_and_share(0)
    send_out(chunks - 1)
    for chunk in range(chunks):
        if chunk + 1 < chunks:
            arrive_and_share(chunk + 1)
        pass_on(chunk)
        if chunk:
            back_keep(chunk - 1).start()
        translate(chunk)
    for chunk in range(chunks):
        if chunk == chunks - 1 and chunks == 1:
            back_keep(chunk).start()
        returned(chunk)
        disaggregate(chunk, chunk == 0, chunk == chunks - 1)
        if chunk == 0 and chunks > 1:
            back_keep(chunks - 1).start()
    give(per_device - 1).start()

    for chunk in range(chunks):

        def finish(step, carry, chunk=chunk):
            there = lax.rem(me + step, samps)
            out_copy(chunk, there, there).wait_send()
            back_copy(chunk, there, there).wait_send()
            return carry

        lax.fori_loop(1, samps, finish, 0)
        for bit, held in plan:
            for mask in held:
                hop(chunk, bit, mask).wait_send()
    for parent in range(per_device):
        give(parent).wait()


def local(
    boxes,
    samps,
    child_out,
    child_octant,
    theta_index,
    theta_weight,
    phi_index,
    phi_weight,
    shift_angle,
    partner_src,
    partner_disp,
    translation,
):
    child_count, parts, samples = child_out.shape
    parents, kids = child_octant.shape
    octant_count, rows2, cols2 = shift_angle.shape
    partners = partner_src.shape[1]
    theta_rows = rows2 // samps
    chunks = cols2 // LANES
    half = NT1 // 2
    width = 2 * NP1
    child = child_out.reshape(child_count, parts, half, width)
    group_rows = parents * samps
    start = lax.axis_index("box") * group_rows
    src_rows = lax.dynamic_slice_in_dim(partner_src, start, group_rows, 0).reshape(-1)
    disp_rows = lax.dynamic_slice_in_dim(partner_disp, start, group_rows, 0).reshape(-1)
    block = (parents, parts, theta_rows, LANES)
    spread = (parents, parts, samps, theta_rows, LANES)
    turns = (octant_count, rows2, LANES)
    anywhere = pl.BlockSpec(memory_space=pl.ANY)
    scalars = pl.BlockSpec(memory_space=pltpu.SMEM)
    vectors = pl.BlockSpec(memory_space=pltpu.VMEM)
    dma = pltpu.SemaphoreType.DMA

    def per_chunk(shape):
        return [pltpu.VMEM(shape, jnp.float32)] * chunks

    child_in = pl.pallas_call(
        functools.partial(step_kernel, boxes, samps, partners),
        out_shape=jax.ShapeDtypeStruct(child.shape, jnp.float32),
        in_specs=[scalars] * 3 + [vectors] * 8 + [anywhere] * 3,
        out_specs=anywhere,
        scratch_shapes=[
            pltpu.VMEM(child.shape, jnp.float32),
            pltpu.VMEM((kids, 3 * NT1, parts * LANES), jnp.bfloat16),
            pltpu.VMEM((2, kids * parts, half, 2 * LANES), jnp.bfloat16),
            pltpu.VMEM((parts, rows2, LANES), jnp.float32),
            pltpu.VMEM((rows2, 3 * NT1), jnp.bfloat16),
            pltpu.VMEM((2 * NT1, rows2), jnp.bfloat16),
        ]
        + per_chunk((boxes, samps) + block)
        + per_chunk(translation.shape[:3] + (LANES,))
        + per_chunk((samps,) + block)
        + per_chunk(spread)
        + per_chunk(spread)
        + per_chunk(turns)
        + per_chunk(turns)
        + [
            dma(()),
            dma((chunks,)),
            dma((parents,)),
            dma((chunks,)),
            dma((chunks,)),
            dma((chunks, samps)),
            dma((chunks, samps)),
            dma((chunks, boxes)),
            dma((chunks, boxes)),
            dma((chunks,)),
            dma((chunks, samps)),
            dma((chunks, samps)),
        ],
        compiler_params=pltpu.CompilerParams(
            collective_id=0, has_side_effects=True, vmem_limit_bytes=VMEM_LIMIT
        ),
    )(
        src_rows,
        disp_rows,
        child_octant.reshape(-1),
        theta_index,
        theta_weight,
        theta_index.T,
        theta_weight.T,
        phi_index,
        phi_weight,
        phi_index.T,
        phi_weight.T,
        child,
        shift_angle,
        translation,
    )
    return child_in.reshape(child_count, parts, samples)


def solution(mesh):
    in_specs = (
        P(("box", "samp"), None, None),
        P(("box", "samp"), None),
        P(),
        P(),
        P(),
        P(),
        P(),
        P(),
        P(),
        P(None, None, "samp", None),
    )
    out_specs = P(("box", "samp"), None, None)
    body = functools.partial(local, mesh.shape["box"], mesh.shape["samp"])
    return jax.shard_map(body, mesh=mesh, in_specs=in_specs, out_specs=out_specs, check_vma=False)
```

```python
import functools

import jax
import jax.numpy as jnp
from jax import lax
from jax.experimental import pallas as pl
from jax.experimental.pallas import tpu as pltpu
from jax.sharding import PartitionSpec as P

NT1 = 96
NP1 = 192
LANES = 128
MESH = pl.DeviceIdType.MESH
VMEM_LIMIT = 62 * 1024 * 1024


def split(values):
    high = values.astype(jnp.bfloat16)
    low = (values - high.astype(jnp.float32)).astype(jnp.bfloat16)
    return high, low


def dot(left, right):
    return jnp.dot(left, right, preferred_element_type=jnp.float32)


def stencil(wanted, index, weight, axis):
    total = jnp.zeros(wanted.shape, jnp.float32)
    for j in range(index.shape[axis]):
        one = slice(j, j + 1)
        spot = (slice(None), one) if axis == 1 else (one, slice(None))
        total = total + jnp.where(wanted == index[spot], weight[spot], 0.0)
    return total


def iota(shape, axis):
    return lax.broadcasted_iota(jnp.int32, shape, axis)


HALF_PI = (1.5703125, 4.837512969970703e-4, 7.54978995489188e-8)


def cos_sin(angle):
    turns = jnp.floor(angle * 0.6366197723675814 + 0.5)
    rest = ((angle - turns * HALF_PI[0]) - turns * HALF_PI[1]) - turns * HALF_PI[2]
    square = rest * rest
    sine = -1.9515295891e-4 * square + 8.3321608736e-3
    sine = (sine * square - 1.6666654611e-1) * square * rest + rest
    cosine = 2.443315711809948e-5 * square - 1.388731625493765e-3
    cosine = (cosine * square + 4.166664568298827e-2) * square * square - 0.5 * square + 1.0
    half = jnp.floor(turns * 0.5)
    odd = turns - 2.0 * half > 0.5
    flip = half - 2.0 * jnp.floor(half * 0.5) > 0.5
    sin_part = jnp.where(odd, cosine, sine)
    cos_part = jnp.where(odd, -sine, cosine)
    return jnp.where(flip, -cos_part, cos_part), jnp.where(flip, -sin_part, sin_part)


def step_kernel(
    boxes,
    samps,
    partners,
    src_rows,
    disp_rows,
    octant,
    theta_index_t,
    theta_weight_t,
    phi_index_t,
    phi_weight_t,
    child,
    angle,
    table,
    result,
    field,
    wide,
    wide_out,
    grid_sum,
    theta_up,
    theta_down,
    *scratch,
):
    count, parts, half, width = child.shape
    chunks = angle.shape[2] // LANES
    rows2 = angle.shape[1]
    sources = scratch[:chunks]
    operators = scratch[chunks : 2 * chunks]
    results = scratch[2 * chunks : 3 * chunks]
    outgoing = scratch[3 * chunks : 4 * chunks]
    incoming = scratch[4 * chunks : 5 * chunks]
    cosines = scratch[5 * chunks : 6 * chunks]
    sines = scratch[6 * chunks : 7 * chunks]
    (
        child_sem,
        angle_sem,
        result_sem,
        load_sem,
        own_sem,
        out_send,
        out_recv,
        box_send,
        box_recv,
        back_own,
        back_send,
        back_recv,
    ) = scratch[7 * chunks :]
    per_device = outgoing[0].shape[0]
    kids = count // per_device
    theta_rows = rows2 // samps
    edge = -(-(width // 2) // LANES) * LANES
    gap = edge - width // 2
    group = lax.axis_index("box")
    me = lax.axis_index("samp")
    bits = [1 << i for i in range(boxes.bit_length() - 1)][::-1]

    def mate(bit):
        return group + bit - 2 * bit * lax.rem(lax.div(group, bit), 2)

    barrier = pltpu.get_barrier_semaphore()
    for step in range(1, samps):
        pl.semaphore_signal(barrier, inc=1, device_id=(group, lax.rem(me + step, samps)), device_id_type=MESH)
    for bit in bits:
        pl.semaphore_signal(barrier, inc=1, device_id=(mate(bit), me), device_id_type=MESH)

    def load(chunk):
        return pltpu.make_async_copy(
            table.at[:, :, :, pl.ds(chunk * LANES, LANES)], operators[chunk], load_sem.at[chunk]
        )

    def keep(chunk):
        return pltpu.make_async_copy(
            outgoing[chunk].at[:, :, me], sources[chunk].at[group, me], own_sem.at[chunk]
        )

    def out_part(chunk, parent, peer):
        return pltpu.make_async_remote_copy(
            src_ref=outgoing[chunk].at[parent, :, peer],
            dst_ref=sources[chunk].at[group, me, parent],
            send_sem=out_send.at[chunk, peer],
            recv_sem=out_recv.at[chunk, me],
            device_id=(group, peer),
            device_id_type=MESH,
        )

    def out_copy(chunk, peer, owner):
        return pltpu.make_async_remote_copy(
            src_ref=outgoing[chunk].at[:, :, peer],
            dst_ref=sources[chunk].at[group, owner],
            send_sem=out_send.at[chunk, peer],
            recv_sem=out_recv.at[chunk, owner],
            device_id=(group, peer),
            device_id_type=MESH,
        )

    def back_slot(chunk, slot):
        return chunk + (slot if chunk == chunks - 1 else 0)

    def back_part(chunk, slot, peer, owner):
        return pltpu.make_async_remote_copy(
            src_ref=results[chunk].at[peer, slot],
            dst_ref=incoming[chunk].at[slot, :, owner],
            send_sem=back_send.at[chunk, peer],
            recv_sem=back_recv.at[back_slot(chunk, slot), owner],
            device_id=(group, peer),
            device_id_type=MESH,
        )

    def back_copy(chunk, peer, owner):
        return pltpu.make_async_remote_copy(
            src_ref=results[chunk].at[peer],
            dst_ref=incoming[chunk].at[:, :, owner],
            send_sem=back_send.at[chunk, peer],
            recv_sem=back_recv.at[chunk, owner],
            device_id=(group, peer),
            device_id_type=MESH,
        )

    def back_keep(chunk):
        return pltpu.make_async_copy(
            results[chunk].at[me], incoming[chunk].at[:, :, me], back_own.at[chunk]
        )

    def box_plan():
        plan = []
        held = [0]
        for bit in bits:
            plan.append((bit, list(held)))
            held = held + [h + bit for h in held]
        return plan

    plan = box_plan()

    def owner_of(mask):
        spot = group
        for bit in bits:
            if mask & bit:
                spot = spot + bit - 2 * bit * lax.rem(lax.div(group, bit), 2)
        return spot

    def hop(chunk, bit, mask):
        return pltpu.make_async_remote_copy(
            src_ref=sources[chunk].at[owner_of(mask)],
            dst_ref=sources[chunk].at[owner_of(mask)],
            send_sem=box_send.at[chunk, mask + bit],
            recv_sem=box_recv.at[chunk, mask + bit],
            device_id=(mate(bit), me),
            device_id_type=MESH,
        )

    def hop_arrival(chunk, mask):
        spot = owner_of(mask)
        return pltpu.make_async_remote_copy(
            src_ref=sources[chunk].at[spot],
            dst_ref=sources[chunk].at[spot],
            send_sem=box_send.at[chunk, mask],
            recv_sem=box_recv.at[chunk, mask],
            device_id=(mate(bits[0]), me),
            device_id_type=MESH,
        )

    def load_angle(chunk):
        return pltpu.make_async_copy(
            angle.at[:, :, pl.ds(chunk * LANES, LANES)], cosines[chunk], angle_sem.at[chunk]
        )

    load_child = pltpu.make_async_copy(child, field, child_sem)

    def give(parent):
        rows = pl.ds(parent * kids, kids)
        return pltpu.make_async_copy(field.at[rows], result.at[rows], result_sem.at[parent])

    def build_theta():
        spot = iota((2 * half, rows2), 0)
        sample = jnp.where(spot < half, 2 * spot, 2 * (spot - half) + 1)
        narrow = stencil(sample, theta_index_t, theta_weight_t, 0)
        high, low = split(narrow.T)
        theta_up[:, : 2 * half] = high
        theta_up[:, 2 * half : 4 * half] = high
        theta_up[:, 4 * half :] = low
        high, low = split(narrow)
        theta_down[: 2 * half] = high
        theta_down[2 * half :] = low

    def turn(chunk):
        def one(spot, carry):
            cos_part, sin_part = cos_sin(cosines[chunk][spot])
            cosines[chunk][spot] = cos_part
            sines[chunk][spot] = sin_part
            return carry

        lax.fori_loop(0, cosines[chunk].shape[0], one, 0)

    def send_out(chunk, parent):
        def one(step, carry):
            out_part(chunk, parent, lax.rem(me + step, samps)).start()
            return carry

        lax.fori_loop(1, samps, one, 0)

    def send_last(chunk):
        send_out(chunk, per_device - 1)
        keep(chunk).start()

    def aggregate(chunk):
        lanes = slice(chunk * LANES, (chunk + 1) * LANES)
        sample = iota((edge, LANES), 0)
        mats = []
        for shift in (0, gap):
            high, low = split(stencil(sample - shift, phi_index_t[:, lanes], phi_weight_t[:, lanes], 0))
            mats.append(jnp.concatenate([high, low], axis=1))

        def one_parent(parent, carry):
            block = field[pl.ds(parent * kids, kids)].reshape(kids * parts * half, width)
            pieces = []
            for mat, start in zip(mats, (0, width - edge)):
                high, low = split(block[:, start : start + edge])
                both = dot(high, mat)
                pieces.append(split(both[:, :LANES] + (both[:, LANES:] + dot(low, mat[:, :LANES]))))
            even, odd = pieces
            for slot, piece in enumerate((even[0], odd[0], even[1], odd[1], even[0], odd[0])):
                piece = piece.reshape(kids, parts, half, LANES)
                for part in range(parts):
                    wide[:, slot * half : (slot + 1) * half, part * LANES : (part + 1) * LANES] = piece[:, part]
            grid_sum[...] = jnp.zeros_like(grid_sum)

            def one_child(kid, inner):
                spot = octant[parent, kid]
                fine = dot(theta_up[...], wide[kid])
                real, imag = fine[:, :LANES], fine[:, LANES:]
                cos_part = cosines[chunk][spot]
                sin_part = sines[chunk][spot]
                grid_sum[0] += real * cos_part - imag * sin_part
                grid_sum[1] += real * sin_part + imag * cos_part
                return inner

            lax.fori_loop(0, kids, one_child, 0)
            for part in range(parts):
                for owner in range(samps):
                    outgoing[chunk][parent, part, owner] = grid_sum[
                        part, owner * theta_rows : (owner + 1) * theta_rows
                    ]

            @pl.when(parent > 0)
            def _():
                send_out(chunk, parent - 1)

            return carry

        lax.fori_loop(0, per_device, one_parent, 0)

    def disaggregate(chunk, first, last):
        rows = slice(chunk * LANES, (chunk + 1) * LANES)
        sample = iota((edge, LANES), 0)
        mats = []
        for shift in (0, gap):
            high, low = split(stencil(sample - shift, phi_index_t[:, rows], phi_weight_t[:, rows], 0).T)
            mats.append((jnp.concatenate([high, high], axis=0), low))

        def one_parent(parent, carry):
            if last:
                returned_part(chunk, parent)
            for part in range(parts):
                for owner in range(samps):
                    grid_sum[part, owner * theta_rows : (owner + 1) * theta_rows] = incoming[chunk][
                        parent, part, owner
                    ]

            def one_child(kid, inner):
                spot = octant[parent, kid]
                real, imag = grid_sum[0], grid_sum[1]
                cos_part = cosines[chunk][spot]
                sin_part = sines[chunk][spot]
                turned = jnp.concatenate(
                    [real * cos_part + imag * sin_part, imag * cos_part - real * sin_part], axis=1
                )
                high, low = split(turned)
                both = dot(theta_down[...], high)
                narrow = both[: 2 * half] + (both[2 * half :] + dot(theta_down[: 2 * half], low))
                for place, piece in enumerate(split(narrow)):
                    for parity in range(2):
                        for part in range(parts):
                            wide_out[
                                parity, kid * parts + part, :, place * LANES : (place + 1) * LANES
                            ] = piece[parity * half : (parity + 1) * half, part * LANES : (part + 1) * LANES]
                return inner

            lax.fori_loop(0, kids, one_child, 0)
            ends = []
            for parity in range(2):
                flat = wide_out[parity].reshape(kids * parts * half, 2 * LANES)
                ends.append(dot(flat, mats[parity][0]) + dot(flat[:, :LANES], mats[parity][1]))
            left, right = ends
            shared = 2 * edge - width
            joined = jnp.concatenate(
                [left[:, : edge - shared], left[:, edge - shared :] + right[:, :shared], right[:, shared:]],
                axis=1,
            ).reshape(kids, parts, half, width)
            spot = pl.ds(parent * kids, kids)
            if first:
                field[spot] = joined
            else:
                field[spot] += joined
            if last:

                @pl.when(parent > 0)
                def _():
                    give(parent - 1).start()

            return carry

        lax.fori_loop(0, per_device, one_parent, 0)

    load_child.start()
    for chunk in range(chunks):
        load_angle(chunk).start()
    for chunk in range(chunks):
        load(chunk).start()
    build_theta()
    load_angle(0).wait()
    turn(0)
    load_child.wait()
    pl.semaphore_wait(barrier, samps - 1 + len(bits))
    aggregate(0)
    for chunk in range(1, chunks):
        load_angle(chunk).wait()
        turn(chunk)
        send_last(chunk - 1)
        aggregate(chunk)

    def arrive_and_share(chunk):
        def arrived(step, carry):
            peer = lax.rem(me + samps - step, samps)
            out_copy(chunk, peer, peer).wait_recv()
            return carry

        keep(chunk).wait()
        lax.fori_loop(1, samps, arrived, 0)
        for bit, held in plan:
            hop(chunk, bit, 0).start()

    def pass_on(chunk):
        for position, (bit, held) in enumerate(plan):
            for mask in held:
                if mask == 0:
                    continue
                hop(chunk, bit, mask).start()
            if position + 1 < len(plan):
                for mask in [h + bit for h in held]:
                    hop_arrival(chunk, mask).wait_recv()

    def translate(chunk):
        last_bit, last_held = plan[-1]
        for mask in [h + last_bit for h in last_held]:
            hop_arrival(chunk, mask).wait_recv()
        load(chunk).wait()

        def receivers(slot, carry):
            def one(step, inner):
                peer = lax.rem(me + 1 + step, samps)
                row = (group * samps + peer) * per_device + slot
                real = jnp.zeros(results[chunk].shape[3:], jnp.float32)
                imag = jnp.zeros(results[chunk].shape[3:], jnp.float32)
                for q in range(partners):
                    source = src_rows[q, row]
                    which = disp_rows[q, row]
                    here = lax.div(source, samps * per_device)
                    rest = lax.rem(source, samps * per_device)
                    from_samp = lax.div(rest, per_device)
                    from_slot = lax.rem(rest, per_device)
                    a = sources[chunk][here, from_samp, from_slot, 0]
                    b = sources[chunk][here, from_samp, from_slot, 1]
                    c = operators[chunk][which, 0]
                    d = operators[chunk][which, 1]
                    real = real + (c * a - d * b)
                    imag = imag + (c * b + d * a)
                results[chunk][peer, slot, 0] = real
                results[chunk][peer, slot, 1] = imag

                @pl.when(step > 0)
                def _():
                    back_part(chunk, slot, lax.rem(me + step, samps), me).start()

                return inner

            lax.fori_loop(0, samps, one, 0)
            return carry

        lax.fori_loop(0, per_device, receivers, 0)

    def returned(chunk):
        def one(step, carry):
            there = lax.rem(me + samps - step, samps)
            back_copy(chunk, there, there).wait_recv()
            return carry

        if chunk < chunks - 1:
            lax.fori_loop(1, samps, one, 0)
        back_keep(chunk).wait()

    def returned_part(chunk, parent):
        def one(step, carry):
            there = lax.rem(me + samps - step, samps)
            back_part(chunk, parent, there, there).wait_recv()
            return carry

        lax.fori_loop(1, samps, one, 0)

    send_last(chunks - 1)
    arrive_and_share(0)
    for chunk in range(chunks):
        if chunk + 1 < chunks:
            arrive_and_share(chunk + 1)
        pass_on(chunk)
        if chunk:
            back_keep(chunk - 1).start()
        translate(chunk)
    for chunk in range(chunks):
        if chunk == chunks - 1 and chunks == 1:
            back_keep(chunk).start()
        returned(chunk)
        disaggregate(chunk, chunk == 0, chunk == chunks - 1)
        if chunk == 0 and chunks > 1:
            back_keep(chunks - 1).start()
    give(per_device - 1).start()

    for chunk in range(chunks):

        def finish(step, carry, chunk=chunk):
            there = lax.rem(me + step, samps)
            out_copy(chunk, there, there).wait_send()
            back_copy(chunk, there, there).wait_send()
            return carry

        lax.fori_loop(1, samps, finish, 0)
        for bit, held in plan:
            for mask in held:
                hop(chunk, bit, mask).wait_send()
    for parent in range(per_device):
        give(parent).wait()


def local(
    boxes,
    samps,
    child_out,
    child_octant,
    theta_index,
    theta_weight,
    phi_index,
    phi_weight,
    shift_angle,
    partner_src,
    partner_disp,
    translation,
):
    child_count, parts, samples = child_out.shape
    parents, kids = child_octant.shape
    octant_count, rows2, cols2 = shift_angle.shape
    partners = partner_src.shape[1]
    theta_rows = rows2 // samps
    chunks = cols2 // LANES
    half = NT1 // 2
    width = 2 * NP1
    child = child_out.reshape(child_count, parts, half, width)
    block = (parents, parts, theta_rows, LANES)
    spread = (parents, parts, samps, theta_rows, LANES)
    turns = (octant_count, rows2, LANES)
    anywhere = pl.BlockSpec(memory_space=pl.ANY)
    scalars = pl.BlockSpec(memory_space=pltpu.SMEM)
    vectors = pl.BlockSpec(memory_space=pltpu.VMEM)
    dma = pltpu.SemaphoreType.DMA

    def per_chunk(shape):
        return [pltpu.VMEM(shape, jnp.float32)] * chunks

    child_in = pl.pallas_call(
        functools.partial(step_kernel, boxes, samps, partners),
        out_shape=jax.ShapeDtypeStruct(child.shape, jnp.float32),
        in_specs=[scalars] * 3 + [vectors] * 4 + [anywhere] * 3,
        out_specs=anywhere,
        scratch_shapes=[
            pltpu.VMEM(child.shape, jnp.float32),
            pltpu.VMEM((kids, 3 * NT1, parts * LANES), jnp.bfloat16),
            pltpu.VMEM((2, kids * parts, half, 2 * LANES), jnp.bfloat16),
            pltpu.VMEM((parts, rows2, LANES), jnp.float32),
            pltpu.VMEM((rows2, 3 * NT1), jnp.bfloat16),
            pltpu.VMEM((2 * NT1, rows2), jnp.bfloat16),
        ]
        + per_chunk((boxes, samps) + block)
        + per_chunk(translation.shape[:3] + (LANES,))
        + per_chunk((samps,) + block)
        + per_chunk(spread)
        + per_chunk(spread)
        + per_chunk(turns)
        + per_chunk(turns)
        + [
            dma(()),
            dma((chunks,)),
            dma((parents,)),
            dma((chunks,)),
            dma((chunks,)),
            dma((chunks, samps)),
            dma((chunks, samps)),
            dma((chunks, boxes)),
            dma((chunks, boxes)),
            dma((chunks,)),
            dma((chunks, samps)),
            dma((chunks - 1 + parents, samps)),
        ],
        compiler_params=pltpu.CompilerParams(
            collective_id=0, has_side_effects=True, vmem_limit_bytes=VMEM_LIMIT
        ),
    )(
        partner_src.T,
        partner_disp.T,
        child_octant,
        theta_index.T,
        theta_weight.T,
        phi_index.T,
        phi_weight.T,
        child,
        shift_angle,
        translation,
    )
    return child_in.reshape(child_count, parts, samples)


def solution(mesh):
    in_specs = (
        P(("box", "samp"), None, None),
        P(("box", "samp"), None),
        P(),
        P(),
        P(),
        P(),
        P(),
        P(),
        P(),
        P(None, None, "samp", None),
    )
    out_specs = P(("box", "samp"), None, None)
    body = functools.partial(local, mesh.shape["box"], mesh.shape["samp"])
    return jax.shard_map(body, mesh=mesh, in_specs=in_specs, out_specs=out_specs, check_vma=False)
```

```python
import functools

import jax
import jax.numpy as jnp
from jax import lax
from jax.experimental import pallas as pl
from jax.experimental.pallas import tpu as pltpu
from jax.sharding import PartitionSpec as P

NT1 = 96
NP1 = 192
LANES = 128
MESH = pl.DeviceIdType.MESH
VMEM_LIMIT = 62 * 1024 * 1024


def split(values):
    high = values.astype(jnp.bfloat16)
    low = (values - high.astype(jnp.float32)).astype(jnp.bfloat16)
    return high, low


def dot(left, right):
    return jnp.dot(left, right, preferred_element_type=jnp.float32)


def stencil(wanted, index, weight, axis):
    total = jnp.zeros(wanted.shape, jnp.float32)
    for j in range(index.shape[axis]):
        one = slice(j, j + 1)
        spot = (slice(None), one) if axis == 1 else (one, slice(None))
        total = total + jnp.where(wanted == index[spot], weight[spot], 0.0)
    return total


def iota(shape, axis):
    return lax.broadcasted_iota(jnp.int32, shape, axis)


HALF_PI = (1.5703125, 4.837512969970703e-4, 7.54978995489188e-8)


def cos_sin(angle):
    turns = jnp.floor(angle * 0.6366197723675814 + 0.5)
    rest = ((angle - turns * HALF_PI[0]) - turns * HALF_PI[1]) - turns * HALF_PI[2]
    square = rest * rest
    sine = -1.9515295891e-4 * square + 8.3321608736e-3
    sine = (sine * square - 1.6666654611e-1) * square * rest + rest
    cosine = 2.443315711809948e-5 * square - 1.388731625493765e-3
    cosine = (cosine * square + 4.166664568298827e-2) * square * square - 0.5 * square + 1.0
    half = jnp.floor(turns * 0.5)
    odd = turns - 2.0 * half > 0.5
    flip = half - 2.0 * jnp.floor(half * 0.5) > 0.5
    sin_part = jnp.where(odd, cosine, sine)
    cos_part = jnp.where(odd, -sine, cosine)
    return jnp.where(flip, -cos_part, cos_part), jnp.where(flip, -sin_part, sin_part)


def step_kernel(
    boxes,
    samps,
    partners,
    src_rows,
    disp_rows,
    octant,
    theta_index_t,
    theta_weight_t,
    phi_index_t,
    phi_weight_t,
    child,
    angle,
    table,
    result,
    field,
    wide,
    wide_out,
    grid_sum,
    theta_up,
    theta_down,
    *scratch,
):
    half = NT1 // 2
    width = 2 * NP1
    chunks = angle.shape[2] // LANES
    rows2 = angle.shape[1]
    sources = scratch[:chunks]
    operators = scratch[chunks : 2 * chunks]
    results = scratch[2 * chunks : 3 * chunks]
    outgoing = scratch[3 * chunks : 4 * chunks]
    incoming = scratch[4 * chunks : 5 * chunks]
    cosines = scratch[5 * chunks : 6 * chunks]
    sines = scratch[6 * chunks : 7 * chunks]
    (
        child_sem,
        angle_sem,
        result_sem,
        load_sem,
        own_sem,
        out_send,
        out_recv,
        box_send,
        box_recv,
        back_own,
        back_send,
        back_recv,
    ) = scratch[7 * chunks :]
    per_device, parts = outgoing[0].shape[:2]
    kids = child.shape[0] // per_device
    per_row = width // LANES
    theta_rows = rows2 // samps
    edge = -(-(width // 2) // LANES) * LANES
    gap = edge - width // 2
    group = lax.axis_index("box")
    me = lax.axis_index("samp")
    bits = [1 << i for i in range(boxes.bit_length() - 1)][::-1]

    def mate(bit):
        return group + bit - 2 * bit * lax.rem(lax.div(group, bit), 2)

    barrier = pltpu.get_barrier_semaphore()
    for step in range(1, samps):
        pl.semaphore_signal(barrier, inc=1, device_id=(group, lax.rem(me + step, samps)), device_id_type=MESH)
    for bit in bits:
        pl.semaphore_signal(barrier, inc=1, device_id=(mate(bit), me), device_id_type=MESH)

    def load(chunk):
        return pltpu.make_async_copy(
            table.at[:, :, :, pl.ds(chunk * LANES, LANES)], operators[chunk], load_sem.at[chunk]
        )

    def keep(chunk):
        return pltpu.make_async_copy(
            outgoing[chunk].at[:, :, me], sources[chunk].at[group, me], own_sem.at[chunk]
        )

    def out_part(chunk, parent, peer):
        return pltpu.make_async_remote_copy(
            src_ref=outgoing[chunk].at[parent, :, peer],
            dst_ref=sources[chunk].at[group, me, parent],
            send_sem=out_send.at[chunk, peer],
            recv_sem=out_recv.at[chunk, me],
            device_id=(group, peer),
            device_id_type=MESH,
        )

    def out_copy(chunk, peer, owner):
        return pltpu.make_async_remote_copy(
            src_ref=outgoing[chunk].at[:, :, peer],
            dst_ref=sources[chunk].at[group, owner],
            send_sem=out_send.at[chunk, peer],
            recv_sem=out_recv.at[chunk, owner],
            device_id=(group, peer),
            device_id_type=MESH,
        )

    def back_slot(chunk, slot):
        return chunk + (slot if chunk == chunks - 1 else 0)

    def back_part(chunk, slot, peer, owner):
        return pltpu.make_async_remote_copy(
            src_ref=results[chunk].at[peer, slot],
            dst_ref=incoming[chunk].at[slot, :, owner],
            send_sem=back_send.at[chunk, peer],
            recv_sem=back_recv.at[back_slot(chunk, slot), owner],
            device_id=(group, peer),
            device_id_type=MESH,
        )

    def back_copy(chunk, peer, owner):
        return pltpu.make_async_remote_copy(
            src_ref=results[chunk].at[peer],
            dst_ref=incoming[chunk].at[:, :, owner],
            send_sem=back_send.at[chunk, peer],
            recv_sem=back_recv.at[chunk, owner],
            device_id=(group, peer),
            device_id_type=MESH,
        )

    def back_keep(chunk):
        return pltpu.make_async_copy(
            results[chunk].at[me], incoming[chunk].at[:, :, me], back_own.at[chunk]
        )

    def box_plan():
        plan = []
        held = [0]
        for bit in bits:
            plan.append((bit, list(held)))
            held = held + [h + bit for h in held]
        return plan

    plan = box_plan()

    def owner_of(mask):
        spot = group
        for bit in bits:
            if mask & bit:
                spot = spot + bit - 2 * bit * lax.rem(lax.div(group, bit), 2)
        return spot

    def hop(chunk, bit, mask):
        return pltpu.make_async_remote_copy(
            src_ref=sources[chunk].at[owner_of(mask)],
            dst_ref=sources[chunk].at[owner_of(mask)],
            send_sem=box_send.at[chunk, mask + bit],
            recv_sem=box_recv.at[chunk, mask + bit],
            device_id=(mate(bit), me),
            device_id_type=MESH,
        )

    def hop_arrival(chunk, mask):
        spot = owner_of(mask)
        return pltpu.make_async_remote_copy(
            src_ref=sources[chunk].at[spot],
            dst_ref=sources[chunk].at[spot],
            send_sem=box_send.at[chunk, mask],
            recv_sem=box_recv.at[chunk, mask],
            device_id=(mate(bits[0]), me),
            device_id_type=MESH,
        )

    def load_angle(chunk):
        return pltpu.make_async_copy(
            angle.at[:, :, pl.ds(chunk * LANES, LANES)], cosines[chunk], angle_sem.at[chunk]
        )

    load_child = pltpu.make_async_copy(child, field, child_sem)

    def tile(parent, part, place):
        return (
            pl.ds(parent * kids, kids),
            pl.ds(place * parts + part, half, stride=per_row * parts),
            slice(None),
        )

    def give(parent):
        rows = pl.ds(parent * kids, kids)
        return pltpu.make_async_copy(field.at[rows], result.at[rows], result_sem.at[parent])

    def build_theta():
        spot = iota((2 * half, rows2), 0)
        sample = jnp.where(spot < half, 2 * spot, 2 * (spot - half) + 1)
        narrow = stencil(sample, theta_index_t, theta_weight_t, 0)
        high, low = split(narrow.T)
        theta_up[:, : 2 * half] = high
        theta_up[:, 2 * half : 4 * half] = high
        theta_up[:, 4 * half :] = low
        high, low = split(narrow)
        theta_down[: 2 * half] = high
        theta_down[2 * half :] = low

    def turn(chunk):
        def one(spot, carry):
            cos_part, sin_part = cos_sin(cosines[chunk][spot])
            cosines[chunk][spot] = cos_part
            sines[chunk][spot] = sin_part
            return carry

        lax.fori_loop(0, cosines[chunk].shape[0], one, 0)

    def send_out(chunk, parent):
        def one(step, carry):
            out_part(chunk, parent, lax.rem(me + step, samps)).start()
            return carry

        lax.fori_loop(1, samps, one, 0)

    def send_last(chunk):
        send_out(chunk, per_device - 1)
        keep(chunk).start()

    def aggregate(chunk):
        lanes = slice(chunk * LANES, (chunk + 1) * LANES)
        sample = iota((edge, LANES), 0)
        mats = []
        for shift in (0, gap):
            high, low = split(stencil(sample - shift, phi_index_t[:, lanes], phi_weight_t[:, lanes], 0))
            mats.append(jnp.concatenate([high, low], axis=1))

        def one_parent(parent, carry):
            block = jnp.concatenate(
                [
                    jnp.concatenate(
                        [field[tile(parent, part, place)].reshape(kids * half, LANES) for place in range(per_row)],
                        axis=1,
                    )
                    for part in range(parts)
                ],
                axis=0,
            )
            pieces = []
            for mat, start in zip(mats, (0, width - edge)):
                high, low = split(block[:, start : start + edge])
                both = dot(high, mat)
                pieces.append(split(both[:, :LANES] + (both[:, LANES:] + dot(low, mat[:, :LANES]))))
            even, odd = pieces
            for slot, piece in enumerate((even[0], odd[0], even[1], odd[1], even[0], odd[0])):
                piece = piece.reshape(parts, kids, half, LANES)
                for part in range(parts):
                    wide[:, slot * half : (slot + 1) * half, part * LANES : (part + 1) * LANES] = piece[part]
            grid_sum[...] = jnp.zeros_like(grid_sum)

            def one_child(kid, inner):
                spot = octant[parent, kid]
                fine = dot(theta_up[...], wide[kid])
                real, imag = fine[:, :LANES], fine[:, LANES:]
                cos_part = cosines[chunk][spot]
                sin_part = sines[chunk][spot]
                grid_sum[0] += real * cos_part - imag * sin_part
                grid_sum[1] += real * sin_part + imag * cos_part
                return inner

            lax.fori_loop(0, kids, one_child, 0)
            for part in range(parts):
                for owner in range(samps):
                    outgoing[chunk][parent, part, owner] = grid_sum[
                        part, owner * theta_rows : (owner + 1) * theta_rows
                    ]

            @pl.when(parent > 0)
            def _():
                send_out(chunk, parent - 1)

            return carry

        lax.fori_loop(0, per_device, one_parent, 0)

    def disaggregate(chunk, first, last):
        rows = slice(chunk * LANES, (chunk + 1) * LANES)
        sample = iota((edge, LANES), 0)
        mats = []
        for shift in (0, gap):
            high, low = split(stencil(sample - shift, phi_index_t[:, rows], phi_weight_t[:, rows], 0).T)
            mats.append((jnp.concatenate([high, high], axis=0), low))

        def one_parent(parent, carry):
            if last:
                returned_part(chunk, parent)
            for part in range(parts):
                for owner in range(samps):
                    grid_sum[part, owner * theta_rows : (owner + 1) * theta_rows] = incoming[chunk][
                        parent, part, owner
                    ]

            def one_child(kid, inner):
                spot = octant[parent, kid]
                real, imag = grid_sum[0], grid_sum[1]
                cos_part = cosines[chunk][spot]
                sin_part = sines[chunk][spot]
                turned = jnp.concatenate(
                    [real * cos_part + imag * sin_part, imag * cos_part - real * sin_part], axis=1
                )
                high, low = split(turned)
                both = dot(theta_down[...], high)
                narrow = both[: 2 * half] + (both[2 * half :] + dot(theta_down[: 2 * half], low))
                for place, piece in enumerate(split(narrow)):
                    for parity in range(2):
                        for part in range(parts):
                            wide_out[
                                parity, kid * parts + part, :, place * LANES : (place + 1) * LANES
                            ] = piece[parity * half : (parity + 1) * half, part * LANES : (part + 1) * LANES]
                return inner

            lax.fori_loop(0, kids, one_child, 0)
            ends = []
            for parity in range(2):
                flat = wide_out[parity].reshape(kids * parts * half, 2 * LANES)
                ends.append(dot(flat, mats[parity][0]) + dot(flat[:, :LANES], mats[parity][1]))
            left, right = ends
            shared = 2 * edge - width
            joined = jnp.concatenate(
                [left[:, : edge - shared], left[:, edge - shared :] + right[:, :shared], right[:, shared:]],
                axis=1,
            ).reshape(kids, parts, half, width)
            for part in range(parts):
                for place in range(per_row):
                    spot = tile(parent, part, place)
                    piece = joined[:, part, :, place * LANES : (place + 1) * LANES]
                    if first:
                        field[spot] = piece
                    else:
                        field[spot] = field[spot] + piece
            if last:

                @pl.when(parent > 0)
                def _():
                    give(parent - 1).start()

            return carry

        lax.fori_loop(0, per_device, one_parent, 0)

    load_child.start()
    for chunk in range(chunks):
        load_angle(chunk).start()
    for chunk in range(chunks):
        load(chunk).start()
    build_theta()
    load_angle(0).wait()
    turn(0)
    load_child.wait()
    pl.semaphore_wait(barrier, samps - 1 + len(bits))
    aggregate(0)
    for chunk in range(1, chunks):
        load_angle(chunk).wait()
        turn(chunk)
        send_last(chunk - 1)
        aggregate(chunk)

    def arrive_and_share(chunk):
        def arrived(step, carry):
            peer = lax.rem(me + samps - step, samps)
            out_copy(chunk, peer, peer).wait_recv()
            return carry

        keep(chunk).wait()
        lax.fori_loop(1, samps, arrived, 0)
        for bit, held in plan:
            hop(chunk, bit, 0).start()

    def pass_on(chunk):
        for position, (bit, held) in enumerate(plan):
            for mask in held:
                if mask == 0:
                    continue
                hop(chunk, bit, mask).start()
            if position + 1 < len(plan):
                for mask in [h + bit for h in held]:
                    hop_arrival(chunk, mask).wait_recv()

    def translate(chunk):
        last_bit, last_held = plan[-1]
        for mask in [h + last_bit for h in last_held]:
            hop_arrival(chunk, mask).wait_recv()
        load(chunk).wait()

        def receivers(slot, carry):
            def one(step, inner):
                peer = lax.rem(me + 1 + step, samps)
                row = (group * samps + peer) * per_device + slot
                real = jnp.zeros(results[chunk].shape[3:], jnp.float32)
                imag = jnp.zeros(results[chunk].shape[3:], jnp.float32)
                for q in range(partners):
                    source = src_rows[q, row]
                    which = disp_rows[q, row]
                    here = lax.div(source, samps * per_device)
                    rest = lax.rem(source, samps * per_device)
                    from_samp = lax.div(rest, per_device)
                    from_slot = lax.rem(rest, per_device)
                    a = sources[chunk][here, from_samp, from_slot, 0]
                    b = sources[chunk][here, from_samp, from_slot, 1]
                    c = operators[chunk][which, 0]
                    d = operators[chunk][which, 1]
                    real = real + (c * a - d * b)
                    imag = imag + (c * b + d * a)
                results[chunk][peer, slot, 0] = real
                results[chunk][peer, slot, 1] = imag

                @pl.when(step > 0)
                def _():
                    back_part(chunk, slot, lax.rem(me + step, samps), me).start()

                return inner

            lax.fori_loop(0, samps, one, 0)
            return carry

        lax.fori_loop(0, per_device, receivers, 0)

    def returned(chunk):
        def one(step, carry):
            there = lax.rem(me + samps - step, samps)
            back_copy(chunk, there, there).wait_recv()
            return carry

        if chunk < chunks - 1:
            lax.fori_loop(1, samps, one, 0)
        back_keep(chunk).wait()

    def returned_part(chunk, parent):
        def one(step, carry):
            there = lax.rem(me + samps - step, samps)
            back_part(chunk, parent, there, there).wait_recv()
            return carry

        lax.fori_loop(1, samps, one, 0)

    send_last(chunks - 1)
    arrive_and_share(0)
    for chunk in range(chunks):
        if chunk + 1 < chunks:
            arrive_and_share(chunk + 1)
        pass_on(chunk)
        if chunk:
            back_keep(chunk - 1).start()
        translate(chunk)
    for chunk in range(chunks):
        if chunk == chunks - 1 and chunks == 1:
            back_keep(chunk).start()
        returned(chunk)
        disaggregate(chunk, chunk == 0, chunk == chunks - 1)
        if chunk == 0 and chunks > 1:
            back_keep(chunks - 1).start()
    give(per_device - 1).start()

    for chunk in range(chunks):

        def finish(step, carry, chunk=chunk):
            there = lax.rem(me + step, samps)
            out_copy(chunk, there, there).wait_send()
            back_copy(chunk, there, there).wait_send()
            return carry

        lax.fori_loop(1, samps, finish, 0)
        for bit, held in plan:
            for mask in held:
                hop(chunk, bit, mask).wait_send()
    for parent in range(per_device):
        give(parent).wait()


def local(
    boxes,
    samps,
    child_out,
    child_octant,
    theta_index,
    theta_weight,
    phi_index,
    phi_weight,
    shift_angle,
    partner_src,
    partner_disp,
    translation,
):
    child_count, parts, samples = child_out.shape
    parents, kids = child_octant.shape
    octant_count, rows2, cols2 = shift_angle.shape
    partners = partner_src.shape[1]
    theta_rows = rows2 // samps
    chunks = cols2 // LANES
    tiles = samples // LANES
    child = child_out.reshape(child_count, parts, tiles, LANES).transpose(0, 2, 1, 3)
    child = child.reshape(child_count, tiles * parts, LANES)
    block = (parents, parts, theta_rows, LANES)
    spread = (parents, parts, samps, theta_rows, LANES)
    turns = (octant_count, rows2, LANES)
    anywhere = pl.BlockSpec(memory_space=pl.ANY)
    scalars = pl.BlockSpec(memory_space=pltpu.SMEM)
    vectors = pl.BlockSpec(memory_space=pltpu.VMEM)
    dma = pltpu.SemaphoreType.DMA

    def per_chunk(shape):
        return [pltpu.VMEM(shape, jnp.float32)] * chunks

    child_in = pl.pallas_call(
        functools.partial(step_kernel, boxes, samps, partners),
        out_shape=jax.ShapeDtypeStruct(child.shape, jnp.float32),
        in_specs=[scalars] * 3 + [vectors] * 4 + [anywhere] * 3,
        out_specs=anywhere,
        scratch_shapes=[
            pltpu.VMEM(child.shape, jnp.float32),
            pltpu.VMEM((kids, 3 * NT1, parts * LANES), jnp.bfloat16),
            pltpu.VMEM((2, kids * parts, NT1 // 2, 2 * LANES), jnp.bfloat16),
            pltpu.VMEM((parts, rows2, LANES), jnp.float32),
            pltpu.VMEM((rows2, 3 * NT1), jnp.bfloat16),
            pltpu.VMEM((2 * NT1, rows2), jnp.bfloat16),
        ]
        + per_chunk((boxes, samps) + block)
        + per_chunk(translation.shape[:3] + (LANES,))
        + per_chunk((samps,) + block)
        + per_chunk(spread)
        + per_chunk(spread)
        + per_chunk(turns)
        + per_chunk(turns)
        + [
            dma(()),
            dma((chunks,)),
            dma((parents,)),
            dma((chunks,)),
            dma((chunks,)),
            dma((chunks, samps)),
            dma((chunks, samps)),
            dma((chunks, boxes)),
            dma((chunks, boxes)),
            dma((chunks,)),
            dma((chunks, samps)),
            dma((chunks - 1 + parents, samps)),
        ],
        compiler_params=pltpu.CompilerParams(
            collective_id=0, has_side_effects=True, vmem_limit_bytes=VMEM_LIMIT
        ),
    )(
        partner_src.T,
        partner_disp.T,
        child_octant,
        theta_index.T,
        theta_weight.T,
        phi_index.T,
        phi_weight.T,
        child,
        shift_angle,
        translation,
    )
    child_in = child_in.reshape(child_count, tiles, parts, LANES).transpose(0, 2, 1, 3)
    return child_in.reshape(child_count, parts, samples)


def solution(mesh):
    in_specs = (
        P(("box", "samp"), None, None),
        P(("box", "samp"), None),
        P(),
        P(),
        P(),
        P(),
        P(),
        P(),
        P(),
        P(None, None, "samp", None),
    )
    out_specs = P(("box", "samp"), None, None)
    body = functools.partial(local, mesh.shape["box"], mesh.shape["samp"])
    return jax.shard_map(body, mesh=mesh, in_specs=in_specs, out_specs=out_specs, check_vma=False)
```
